32 devices in a mesh: grp: 2 (over y), skill: 16 (over z, x, core).
Axes of the slice: x: 2, y: 2, z: 4, core: 2. Of those that a mesh axis runs over, the one named last changes fastest.
Arguments:
- value_next: bfloat16 [2048, 4, 2048], P('skill', 'grp'), parts along dimension 1, may hold values from -6 to 6
- income_matrix: float32 [64, 32], P('grp'), parts along dimension 0, may hold values from -1 to 1
- block_weights: bfloat16 [16, 16, 4, 128, 128], P('skill')
- block_offset: int32 [16, 16, 4], P('skill'), may hold values from 0 to 3, as said below
- block_count: int32 [16, 16], P('skill'), may hold values from 1 to 4, as said below
- asset_next: int32 [16, 2, 2048], replicated, may hold values from 0 to 1
- flow: float32 [32, 2, 2048], P('grp'), parts along dimension 0, may hold values from -4 to 15
Outputs:
- value_now: bfloat16 [2048, 4, 2048], P('skill', 'grp'), parts along dimension 1
The draws below stay inside these ranges and needn't reach their ends.
There are 2 independent parts, one for each index of `grp`. The reference program is written for one: setup_inputs(seed, part) draws one part's arguments, and reference() takes and returns one part's arrays. A program takes and returns all parts, laid end to end along the dimension named above; an argument that names none is the same for every part. Nothing has to cross between parts.
Inputs may be any that keep to these rules, and one draw needn't show every extreme that they name: `block_offset`: each row of 4 entries is a permutation of 0 to 3, the same for every level. `block_count`: the same for every level.
All inputs are finite; a program needn't handle non-finite values.
Results may differ from the reference program's by a relative error of at most 0.0031.
Values may be sent and summed in bfloat16 or wider, within the bound.
A program may use at most 128 MiB of HBM per device.

```python
import jax
import jax.numpy as jnp
from jax import lax

TILE = 128
H = 64
E = 32
INVEST = 16
BLOCKS = 4
A = 2
TILES = 16
SKILLS = 2048
HE = 2048


def draw_flow(key, part):
    base_key = jax.random.fold_in(key, 11)
    noise_key = jax.random.fold_in(key, 14)
    spread_key = jax.random.fold_in(key, 15)
    shape = (INVEST, A, H * E)
    spread = jnp.exp(jax.random.uniform(spread_key, (1, 1, H * E), jnp.float32, jnp.log(0.005), jnp.log(0.5)))
    base = jnp.clip(jax.random.normal(base_key, (1, A, H * E), jnp.float32), -3.5, 3.5)
    noise = jnp.clip(jax.random.normal(noise_key, shape, jnp.float32), -1.0, 1.0)
    return base + spread * noise


def draw_block_weights(key, part):
    common_key = jax.random.fold_in(key, 21)
    level_key = jax.random.fold_in(key, 22)
    factor = (BLOCKS * TILE) ** (-0.5)
    common = jnp.clip(jax.random.normal(common_key, (TILES, 1, BLOCKS, TILE, TILE), jnp.float32), -6.0, 6.0)
    level = jnp.clip(jax.random.normal(level_key, (TILES, INVEST, BLOCKS, TILE, TILE), jnp.float32), -6.0, 6.0)
    return ((common + 0.075 * level) * factor).astype(jnp.bfloat16)


def draw_block_offset(key, part):
    rank_key = jax.random.fold_in(key, 31)
    ranks = jax.random.randint(rank_key, (TILES, BLOCKS), 0, 1 << 20) * BLOCKS + jnp.arange(BLOCKS, dtype=jnp.int32)[None, :]
    order = jnp.argsort(ranks, axis=-1, stable=True).astype(jnp.int32)
    return jnp.broadcast_to(order[:, None, :], (TILES, INVEST, BLOCKS)).astype(jnp.int32)


def draw_block_count(key, part):
    count_key = jax.random.fold_in(key, 41)
    top_key = jax.random.fold_in(key, 42)
    step_key = jax.random.fold_in(key, 43)
    counts = jax.random.randint(count_key, (TILES,), 1, BLOCKS + 1)
    top_pos = jax.random.randint(top_key, (), 0, TILES)
    low_pos = (top_pos + 1 + jax.random.randint(step_key, (), 0, TILES - 1)) % TILES
    places = jnp.arange(TILES, dtype=jnp.int32)
    counts = jnp.where(places == top_pos, BLOCKS, counts)
    counts = jnp.where(places == low_pos, 1, counts)
    return jnp.broadcast_to(counts[:, None], (TILES, INVEST)).astype(jnp.int32)


def plant(values, key, least, largest):
    index_at = [jax.random.randint(jax.random.fold_in(key, axis), (), 0, length) for axis, length in enumerate(values.shape)]
    widest = values.shape.index(max(values.shape))
    next_to = index_at[:widest] + [(index_at[widest] + 1) % values.shape[widest]] + index_at[widest + 1:]
    return values.at[tuple(index_at)].set(least).at[tuple(next_to)].set(largest)


def shard_levels(own_key, shape, pieces, low, top_value):
    level, own = 1.0, jax.random.fold_in(own_key, 6)
    for dim, parts in pieces:
        steps = jnp.exp(jax.random.uniform(jax.random.fold_in(own, dim), (parts,), jnp.float32, low / len(pieces), top_value / len(pieces)))
        level = level * jnp.repeat(steps, shape[dim] // parts).reshape([-1 if axis == dim else 1 for axis in range(len(shape))])
    return level


def scatter_about(stream_key, dims, width, reach, cuts=(), kind=jnp.bfloat16):
    drawn = width * jax.random.normal(stream_key, dims, jnp.float32)
    if cuts:
        drawn = drawn * shard_levels(stream_key, dims, cuts, -0.22, 0.18)
    return jnp.clip(drawn, -reach, reach).astype(kind)


def setup_inputs(seed: int = 0, part: int = 0) -> dict:
    arg_keys = jax.random.split(jax.random.key(seed), 8)
    part_keys = jax.random.split(jax.random.fold_in(arg_keys[7], part), 8)
    return {
        "value_next": scatter_about(part_keys[0], (HE, A, SKILLS), 1.0, 6.0, ((0, 16),)),
        "income_matrix": scatter_about(part_keys[1], (E, E), E ** -0.5, 1.0, (), jnp.float32),
        "block_weights": draw_block_weights(jax.random.fold_in(arg_keys[7], 71), part),
        "block_offset": draw_block_offset(jax.random.fold_in(arg_keys[7], 71), part),
        "block_count": draw_block_count(jax.random.fold_in(arg_keys[7], 71), part),
        "asset_next": plant(jax.random.randint(arg_keys[5], (INVEST, A, HE), 0, A), jax.random.fold_in(arg_keys[5], 1), 0, A - 1).astype(jnp.int32),
        "flow": draw_flow(jax.random.fold_in(jax.random.fold_in(arg_keys[7], part), 71), part),
    }


def reference(value_next, income_matrix, block_weights, block_offset, block_count, asset_next, flow):
    rows = H * E
    grid = value_next.astype(jnp.float32).reshape(H, E, A * SKILLS)
    mixed = jnp.einsum("fe,hex->hfx", income_matrix, grid, precision=lax.Precision.HIGHEST)
    expected = mixed.reshape(rows, A, SKILLS).astype(jnp.bfloat16)
    padded = jnp.pad(expected, ((0, 0), (0, 0), (0, (BLOCKS - 1) * TILE)))
    place = jnp.arange(BLOCKS, dtype=jnp.int32)
    flow_rows = jnp.transpose(flow, (0, 2, 1))[..., None]
    choose = jnp.transpose(asset_next, (0, 2, 1))

    def one_tile(tile_id):
        start = (tile_id * TILE).astype(jnp.int32)
        window = lax.dynamic_slice_in_dim(padded, start, BLOCKS * TILE, 2).reshape(rows * A, BLOCKS * TILE)
        offsets = block_offset[tile_id]
        counts = block_count[tile_id]
        select = ((offsets[:, :, None] == place[None, None, :]) & (place[None, :, None] < counts[:, None, None])).astype(jnp.float32)
        stacked = jnp.einsum("ikr,ikst->irts", select, block_weights[tile_id].astype(jnp.float32))
        stacked = stacked.astype(jnp.bfloat16).reshape(INVEST, BLOCKS * TILE, TILE)

        def level(index):
            cont = jnp.dot(window, stacked[index], preferred_element_type=jnp.float32).reshape(rows, A, TILE)
            where = jnp.broadcast_to(choose[index][:, :, None], (rows, A, TILE))
            picked = jnp.take_along_axis(cont, where, axis=1)
            return (flow_rows[index] + 0.96 * picked) / 0.05

        scores = lax.map(level, jnp.arange(INVEST, dtype=jnp.int32))
        return (0.05 * jax.nn.logsumexp(scores, axis=0)).astype(jnp.bfloat16)

    result = lax.map(one_tile, jnp.arange(TILES, dtype=jnp.int32))
    return jnp.transpose(result, (1, 2, 0, 3)).reshape(rows, A, SKILLS)
```

```python
import functools
import math

import jax
import jax.numpy as jnp
from jax import lax
from jax.experimental import pallas as pl
from jax.experimental.pallas import tpu as pltpu
from jax.sharding import PartitionSpec as P

def shifted(block, axis, distance):
    devices = range(lax.axis_size(axis))
    route = [(i - distance, i) for i in devices if i - distance in devices]
    return lax.ppermute(block, axis, route)


def on_device_split(
    value_next, income_matrix, block_weights, block_offset, block_count, asset_next, flow
):
    tiles = lax.axis_size("skill")
    local_rows, assets, skills = value_next.shape
    tile = skills // tiles
    rows = local_rows * tiles
    shocks = income_matrix.shape[0]
    parents = rows // shocks
    blocks = block_offset.shape[-1]
    levels = block_offset.shape[1]
    arrived = lax.all_to_all(value_next, "skill", split_axis=2, concat_axis=0, tiled=True)
    width = arrived.shape[2]
    grid = arrived.astype(jnp.float32).reshape(parents, shocks, assets * width)
    mixed = jnp.einsum("fe,hex->hfx", income_matrix, grid, precision=lax.Precision.HIGHEST)
    own_tile = mixed.reshape(rows, assets, width).astype(jnp.bfloat16)
    gathered = [own_tile]
    for step in range(1, blocks):
        gathered.append(shifted(own_tile, "skill", -step))
    window = jnp.concatenate(gathered, axis=2)
    matrix = window.reshape(rows * assets, blocks * tile)
    place = jnp.arange(blocks, dtype=jnp.int32)
    offsets = block_offset[0]
    counts = block_count[0]
    select = (
        (offsets[:, :, None] == place[None, None, :])
        & (place[None, :, None] < counts[:, None, None])
    ).astype(jnp.float32)
    transit = jnp.einsum("ikr,ikst->irts", select, block_weights[0].astype(jnp.float32))
    transit = transit.astype(jnp.bfloat16).reshape(levels, blocks * tile, tile)
    flow_rows = jnp.transpose(flow, (0, 2, 1))[..., None]
    choose = jnp.transpose(asset_next, (0, 2, 1))

    def level_step(index, carry):
        running_max, running_total = carry
        cont = jnp.dot(matrix, transit[index], preferred_element_type=jnp.float32).reshape(
            rows, assets, tile
        )
        chosen = choose[index][:, :, None]
        picked = jnp.zeros((rows, assets, tile), jnp.float32)
        for option in range(assets):
            picked = picked + jnp.where(chosen == option, cont[:, option : option + 1, :], 0.0)
        score = (flow_rows[index] + 0.96 * picked) / 0.05
        new_max = jnp.maximum(running_max, score)
        new_total = running_total * jnp.exp(running_max - new_max) + jnp.exp(score - new_max)
        return (new_max, new_total)

    start_max = jnp.full((rows, assets, tile), -jnp.inf, jnp.float32)
    start_total = jnp.zeros((rows, assets, tile), jnp.float32)
    final_max, final_total = lax.fori_loop(0, levels, level_step, (start_max, start_total))
    value_tile = (0.05 * (final_max + jnp.log(final_total))).astype(jnp.bfloat16)
    return lax.all_to_all(value_tile, "skill", split_axis=0, concat_axis=2, tiled=True)


SUB = 16
STEP = 32
SCALE = math.log2(math.e) / 0.05


def split_three(mix):
    high = mix.astype(jnp.bfloat16)
    rest = mix - high.astype(jnp.float32)
    middle = rest.astype(jnp.bfloat16)
    low = (rest - middle.astype(jnp.float32)).astype(jnp.bfloat16)
    return high, middle, low


def arrange_weights(t, tiles, weights, offsets, counts, sorted_weights):
    levels, blocks, tile, _ = weights.shape

    def one_level(i, carry):
        for r in range(blocks):
            total = jnp.zeros((tile, tile), jnp.float32)
            for k in range(blocks):
                live = (offsets[k] == r) & (counts > k) & (t + r < tiles)
                total = total + jnp.where(live, weights[i, k].astype(jnp.float32), 0.0)
            total = total.astype(jnp.bfloat16)
            for q in range(tile // STEP):
                sorted_weights[q, pl.ds(pl.multiple_of(i * STEP, STEP), STEP), r * tile : (r + 1) * tile] = total[
                    q * STEP : (q + 1) * STEP
                ]
        return carry

    lax.fori_loop(0, levels, one_level, 0)


def one_chunk(window, flow, choose, sorted_weights, scaled, chosen, cont, value, levels, rows):
    for a in range(2):
        scaled[a] = flow[:, a, :] * SCALE
        chosen[a] = choose[:, a, :]
    steps = sorted_weights.shape[0]

    def multiply(q):
        cont[q % 2] = lax.dot_general(
            sorted_weights[q], window, (((1,), (1,)), ((), ())), preferred_element_type=jnp.float32
        )

    def reduce(q):
        for part in range(STEP // SUB):
            for a in range(2):
                scores = []
                for i in range(levels):
                    at = i * STEP + part * SUB
                    first = cont[q % 2, at : at + SUB, :rows]
                    second = cont[q % 2, at : at + SUB, rows:]
                    picked = jnp.where(chosen[a, i : i + 1, :] == 1, second, first)
                    scores.append(scaled[a, i : i + 1, :] + (0.96 * SCALE) * picked)
                top = scores
                while len(top) > 1:
                    top = [jnp.maximum(x, y) for x, y in zip(top[::2], top[1::2])]
                terms = [jnp.exp2(x - top[0]) for x in scores]
                while len(terms) > 1:
                    terms = [x + y for x, y in zip(terms[::2], terms[1::2])]
                start = q * STEP + part * SUB
                value[a, start : start + SUB, :] = (1.0 / SCALE) * (top[0] + jnp.log2(terms[0]))

    multiply(0)
    for q in range(steps):
        if q + 1 < steps:
            multiply(q + 1)
        reduce(q)

def mix_kernel(mix, values, out):
    tile = out.shape[-1]
    parts = split_three(mix[...])
    for t in range(out.shape[0]):
        block = values[:, t * tile : (t + 1) * tile]
        total = jnp.dot(parts[2], block, preferred_element_type=jnp.float32)
        total = total + jnp.dot(parts[1], block, preferred_element_type=jnp.float32)
        total = total + jnp.dot(parts[0], block, preferred_element_type=jnp.float32)
        out[t, 0] = total.astype(jnp.bfloat16)


def level_kernel(
    tiles, offsets, counts, weights, flow, choose, w0, w1, w2, w3, out, sorted_weights, scaled, chosen, cont, value
):
    levels = weights.shape[0]
    rows = w0.shape[2]
    tile = w0.shape[3]

    @pl.when(pl.program_id(0) == 0)
    def _():
        t = lax.axis_index("skill")
        arrange_weights(t, tiles, weights, [offsets[0, k] for k in range(4)], counts[0, 0], sorted_weights)

    window = jnp.concatenate([w[0].reshape(2 * rows, tile) for w in (w0, w1, w2, w3)], axis=1)
    one_chunk(window, flow[...], choose[...], sorted_weights, scaled, chosen, cont, value, levels, rows)
    for a in range(2):
        out[0, a] = value[a].T.astype(jnp.bfloat16)


def on_device(value_next, income_matrix, block_weights, block_offset, block_count, asset_next, flow):
    tiles = lax.axis_size("skill")
    rows, assets, skills = value_next.shape
    tile = skills // tiles
    shocks = income_matrix.shape[0]
    levels, blocks = block_weights.shape[1:3]
    mix = jnp.kron(jnp.eye(rows // shocks, dtype=jnp.float32), income_matrix)
    turned = jnp.transpose(value_next, (1, 0, 2))
    expected = pl.pallas_call(
        mix_kernel,
        out_shape=jax.ShapeDtypeStruct((tiles, assets, rows, tile), jnp.bfloat16),
        grid=(assets,),
        in_specs=[
            pl.BlockSpec((rows, rows), lambda a: (0, 0)),
            pl.BlockSpec((None, rows, skills), lambda a: (a, 0, 0)),
        ],
        out_specs=pl.BlockSpec((tiles, 1, rows, tile), lambda a: (0, a, 0, 0)),
    )(mix, turned)
    own = lax.all_to_all(expected, "skill", split_axis=0, concat_axis=0, tiled=True)
    window = [own] + [shifted(own, "skill", -step) for step in range(1, blocks)]
    chunk = pl.BlockSpec((1, assets, rows, tile), lambda n: (n, 0, 0, 0))
    per_row = pl.BlockSpec((levels, assets, rows), lambda n: (0, 0, n))
    value = pl.pallas_call(
        functools.partial(level_kernel, tiles),
        out_shape=jax.ShapeDtypeStruct((tiles, assets, rows, tile), jnp.bfloat16),
        grid=(tiles,),
        in_specs=[
            pl.BlockSpec(memory_space=pltpu.SMEM),
            pl.BlockSpec(memory_space=pltpu.SMEM),
            pl.BlockSpec((levels, blocks, tile, tile), lambda n: (0, 0, 0, 0)),
            per_row,
            per_row,
            chunk,
            chunk,
            chunk,
            chunk,
        ],
        out_specs=chunk,
        scratch_shapes=[
            pltpu.VMEM((tile // STEP, levels * STEP, blocks * tile), jnp.bfloat16),
            pltpu.VMEM((assets, levels, rows), jnp.float32),
            pltpu.VMEM((assets, levels, rows), jnp.int32),
            pltpu.VMEM((2, levels * STEP, assets * rows), jnp.float32),
            pltpu.VMEM((assets, tile, rows), jnp.float32),
        ],
        compiler_params=pltpu.CompilerParams(vmem_limit_bytes=48 * 1024 * 1024),
    )(block_offset[0], block_count, block_weights[0], flow, asset_next, *window)
    back = lax.all_to_all(value, "skill", split_axis=0, concat_axis=0, tiled=True)
    return jnp.transpose(back, (2, 1, 0, 3)).reshape(rows, assets, skills)


def solution(mesh):
    placed = (
        P("skill", "grp", None),
        P("grp", None),
        P("skill", None, None, None, None),
        P("skill", None, None),
        P("skill", None),
        P(),
        P("grp", None, None),
    )

    def body(value_next, income_matrix, *rest):
        whole = value_next.shape[0] % income_matrix.shape[0] == 0
        return (on_device if whole else on_device_split)(value_next, income_matrix, *rest)

    return jax.shard_map(
        body, mesh=mesh, in_specs=placed, out_specs=P("skill", "grp", None), check_vma=False
    )
```

```python
import functools
import math

import jax
import jax.numpy as jnp
from jax import lax
from jax.experimental import pallas as pl
from jax.experimental.pallas import tpu as pltpu
from jax.sharding import PartitionSpec as P

def shifted(block, axis, distance):
    devices = range(lax.axis_size(axis))
    route = [(i - distance, i) for i in devices if i - distance in devices]
    return lax.ppermute(block, axis, route)


def on_device_split(
    value_next, income_matrix, block_weights, block_offset, block_count, asset_next, flow
):
    tiles = lax.axis_size("skill")
    local_rows, assets, skills = value_next.shape
    tile = skills // tiles
    rows = local_rows * tiles
    shocks = income_matrix.shape[0]
    parents = rows // shocks
    blocks = block_offset.shape[-1]
    levels = block_offset.shape[1]
    arrived = lax.all_to_all(value_next, "skill", split_axis=2, concat_axis=0, tiled=True)
    width = arrived.shape[2]
    grid = arrived.astype(jnp.float32).reshape(parents, shocks, assets * width)
    mixed = jnp.einsum("fe,hex->hfx", income_matrix, grid, precision=lax.Precision.HIGHEST)
    own_tile = mixed.reshape(rows, assets, width).astype(jnp.bfloat16)
    gathered = [own_tile]
    for step in range(1, blocks):
        gathered.append(shifted(own_tile, "skill", -step))
    window = jnp.concatenate(gathered, axis=2)
    matrix = window.reshape(rows * assets, blocks * tile)
    place = jnp.arange(blocks, dtype=jnp.int32)
    offsets = block_offset[0]
    counts = block_count[0]
    select = (
        (offsets[:, :, None] == place[None, None, :])
        & (place[None, :, None] < counts[:, None, None])
    ).astype(jnp.float32)
    transit = jnp.einsum("ikr,ikst->irts", select, block_weights[0].astype(jnp.float32))
    transit = transit.astype(jnp.bfloat16).reshape(levels, blocks * tile, tile)
    flow_rows = jnp.transpose(flow, (0, 2, 1))[..., None]
    choose = jnp.transpose(asset_next, (0, 2, 1))

    def level_step(index, carry):
        running_max, running_total = carry
        cont = jnp.dot(matrix, transit[index], preferred_element_type=jnp.float32).reshape(
            rows, assets, tile
        )
        chosen = choose[index][:, :, None]
        picked = jnp.zeros((rows, assets, tile), jnp.float32)
        for option in range(assets):
            picked = picked + jnp.where(chosen == option, cont[:, option : option + 1, :], 0.0)
        score = (flow_rows[index] + 0.96 * picked) / 0.05
        new_max = jnp.maximum(running_max, score)
        new_total = running_total * jnp.exp(running_max - new_max) + jnp.exp(score - new_max)
        return (new_max, new_total)

    start_max = jnp.full((rows, assets, tile), -jnp.inf, jnp.float32)
    start_total = jnp.zeros((rows, assets, tile), jnp.float32)
    final_max, final_total = lax.fori_loop(0, levels, level_step, (start_max, start_total))
    value_tile = (0.05 * (final_max + jnp.log(final_total))).astype(jnp.bfloat16)
    return lax.all_to_all(value_tile, "skill", split_axis=0, concat_axis=2, tiled=True)


SUB = 16
STEP = 32
SCALE = math.log2(math.e) / 0.05


def split_three(mix):
    high = mix.astype(jnp.bfloat16)
    rest = mix - high.astype(jnp.float32)
    middle = rest.astype(jnp.bfloat16)
    low = (rest - middle.astype(jnp.float32)).astype(jnp.bfloat16)
    return high, middle, low


def arrange_weights(t, tiles, weights, offsets, counts, sorted_weights):
    levels, blocks, tile, _ = weights.shape

    def one_level(i, carry):
        for r in range(blocks):
            total = jnp.zeros((tile, tile), jnp.float32)
            for k in range(blocks):
                live = (offsets[k] == r) & (counts > k) & (t + r < tiles)
                total = total + jnp.where(live, weights[i, k].astype(jnp.float32), 0.0)
            total = total.astype(jnp.bfloat16)
            for q in range(tile // STEP):
                sorted_weights[q, pl.ds(pl.multiple_of(i * STEP, STEP), STEP), r * tile : (r + 1) * tile] = total[
                    q * STEP : (q + 1) * STEP
                ]
        return carry

    lax.fori_loop(0, levels, one_level, 0)


def one_chunk(window, flow, choose, sorted_weights, scaled, chosen, cont, value, levels, rows):
    for a in range(2):
        scaled[a] = flow[:, a, :] * SCALE
        chosen[a] = choose[:, a, :]
    steps = sorted_weights.shape[0]

    def multiply(q):
        cont[q % 2] = lax.dot_general(
            sorted_weights[q], window, (((1,), (1,)), ((), ())), preferred_element_type=jnp.float32
        )

    def reduce(q):
        for part in range(STEP // SUB):
            for a in range(2):
                scores = []
                for i in range(levels):
                    at = i * STEP + part * SUB
                    first = cont[q % 2, at : at + SUB, :rows]
                    second = cont[q % 2, at : at + SUB, rows:]
                    picked = jnp.where(chosen[a, i : i + 1, :] == 1, second, first)
                    scores.append(scaled[a, i : i + 1, :] + (0.96 * SCALE) * picked)
                top = scores
                while len(top) > 1:
                    top = [jnp.maximum(x, y) for x, y in zip(top[::2], top[1::2])]
                terms = [jnp.exp2(x - top[0]) for x in scores]
                while len(terms) > 1:
                    terms = [x + y for x, y in zip(terms[::2], terms[1::2])]
                start = q * STEP + part * SUB
                value[a, start : start + SUB, :] = (1.0 / SCALE) * (top[0] + jnp.log2(terms[0]))

    multiply(0)
    for q in range(steps):
        if q + 1 < steps:
            multiply(q + 1)
        reduce(q)

MESH = pl.DeviceIdType.MESH


def fused_kernel(
    tiles,
    offsets,
    counts,
    mix,
    values,
    weights,
    flow,
    choose,
    out,
    expected,
    window,
    sorted_weights,
    results,
    scaled,
    chosen,
    cont,
    value,
    in_send,
    in_recv,
    one_send,
    one_recv,
    two_send,
    two_recv,
    out_send,
    out_recv,
    weight_sems,
    local_sem,
):
    chips = tiles // 2
    levels, blocks, tile, _ = weights.shape
    rows = values.shape[1]
    me = lax.axis_index("skill")
    chip = lax.div(me, 2)
    core = lax.rem(me, 2)
    partner = chip * 2 + 1 - core

    def device(at):
        return {"skill": at * 2 + core}

    def source(step):
        return lax.rem(chip + step, chips)

    barrier = pltpu.get_barrier_semaphore()

    def greet(step, carry):
        pl.semaphore_signal(barrier, inc=1, device_id=device(source(step)), device_id_type=MESH)
        return carry

    lax.fori_loop(1, chips, greet, 0)
    pl.semaphore_signal(barrier, inc=1, device_id={"skill": partner}, device_id_type=MESH)

    parts = split_three(mix[...])

    def mixed(target, a):
        block = values[a, :, pl.ds(pl.multiple_of(target * 2 * tile, 2 * tile), 2 * tile)]
        total = jnp.dot(parts[2], block, preferred_element_type=jnp.float32)
        total = total + jnp.dot(parts[1], block, preferred_element_type=jnp.float32)
        total = total + jnp.dot(parts[0], block, preferred_element_type=jnp.float32)
        return total.astype(jnp.bfloat16)

    def in_copy(target, origin):
        return pltpu.make_async_remote_copy(
            src_ref=expected.at[target],
            dst_ref=window.at[origin, pl.ds(0, 2)],
            send_sem=in_send.at[target],
            recv_sem=in_recv.at[origin],
            device_id=device(target),
            device_id_type=MESH,
        )

    def one_copy(at):
        return pltpu.make_async_remote_copy(
            src_ref=window.at[at, pl.ds(0, 2)],
            dst_ref=window.at[at, pl.ds(2, 2)],
            send_sem=one_send.at[at],
            recv_sem=one_recv.at[at],
            device_id=device(lax.rem(chip + chips - 1, chips)),
            device_id_type=MESH,
        )

    def two_copy(at):
        return pltpu.make_async_remote_copy(
            src_ref=window.at[at, 0],
            dst_ref=window.at[at, 4],
            send_sem=two_send.at[at],
            recv_sem=two_recv.at[at],
            device_id=device(lax.rem(chip + chips - 2, chips)),
            device_id_type=MESH,
        )

    def out_copy(target, origin):
        return pltpu.make_async_remote_copy(
            src_ref=results.at[target],
            dst_ref=out.at[pl.ds(origin * 2, 2)],
            send_sem=out_send.at[target],
            recv_sem=out_recv.at[origin],
            device_id=device(target),
            device_id_type=MESH,
        )

    def weight_copy(which):
        return pltpu.make_async_remote_copy(
            src_ref=sorted_weights.at[which],
            dst_ref=sorted_weights.at[which],
            send_sem=weight_sems.at[0],
            recv_sem=weight_sems.at[1],
            device_id={"skill": partner},
            device_id_type=MESH,
        )

    pl.semaphore_wait(barrier, chips)

    def send_in(step, carry):
        target = lax.rem(chip + chips - step, chips)
        for a in range(2):
            total = mixed(target, a)
            expected[target, 0, a] = total[:, :tile]
            expected[target, 1, a] = total[:, tile:]
        in_copy(target, chip).start()
        return carry

    lax.fori_loop(1, chips, send_in, 0)
    for a in range(2):
        total = mixed(chip, a)
        window[chip, 0, a] = total[:, :tile]
        window[chip, 1, a] = total[:, tile:]

    @pl.when(chip + 1 >= chips)
    def _():
        def clear(at, carry):
            for slot in (2, 3):
                window[at, slot] = jnp.zeros(window.shape[2:], jnp.bfloat16)
            return carry

        lax.fori_loop(0, chips, clear, 0)

    @pl.when(chip + 2 >= chips)
    def _():
        def clear(at, carry):
            window[at, 4] = jnp.zeros(window.shape[2:], jnp.bfloat16)
            return carry

        lax.fori_loop(0, chips, clear, 0)

    def relay(at):
        @pl.when(chip >= 1)
        def _():
            one_copy(at).start()

        @pl.when(chip >= 2)
        def _():
            two_copy(at).start()

    relay(chip)
    arrange_weights(
        me, tiles, weights, [offsets[0, k] for k in range(blocks)], counts[0, 0], sorted_weights.at[core]
    )
    weight_copy(core).start()

    def arrive(step):
        at = source(step)
        in_copy(lax.rem(chip + 1, chips), at).wait_recv()
        relay(at)

    arrive(1)
    arrive(2)
    weight_copy(1 - core).wait_recv()

    def compute(step, carry):
        at = source(step + 2)

        @pl.when(step + 3 < chips)
        def _():
            arrive(step + 3)

        @pl.when(chip + 1 < chips)
        def _():
            one_copy(at).wait_recv()

        @pl.when(chip + 2 < chips)
        def _():
            two_copy(at).wait_recv()

        start = pl.multiple_of((at * 2 + core) * rows, rows)
        flow_here = flow[:, :, pl.ds(start, rows)]
        choose_here = choose[:, :, pl.ds(start, rows)]

        def one_tile(t, inner):
            blocks_here = [window[at, t + r].reshape(2 * rows, tile) for r in range(blocks)]
            one_chunk(
                jnp.concatenate(blocks_here, axis=1),
                flow_here,
                choose_here,
                sorted_weights.at[t],
                scaled,
                chosen,
                cont,
                value,
                levels,
                rows,
            )
            for a in range(2):
                results[at, t, a] = value[a].T.astype(jnp.bfloat16)
            return inner

        lax.fori_loop(0, 2, one_tile, 0)

        @pl.when(at != chip)
        def _():
            out_copy(at, chip).start()

        @pl.when(at == chip)
        def _():
            pltpu.make_async_copy(results.at[chip], out.at[pl.ds(chip * 2, 2)], local_sem).start()

        return carry

    lax.fori_loop(0, chips, compute, 0)

    pltpu.make_async_copy(results.at[chip], out.at[pl.ds(chip * 2, 2)], local_sem).wait()
    weight_copy(core).wait_send()

    def finish(step, carry):
        at = source(step)
        in_copy(at, chip).wait_send()
        out_copy(at, chip).wait_send()
        out_copy(at, at).wait_recv()
        return carry

    lax.fori_loop(1, chips, finish, 0)

    def relayed(at, carry):
        @pl.when(chip >= 1)
        def _():
            one_copy(at).wait_send()

        @pl.when(chip >= 2)
        def _():
            two_copy(at).wait_send()

        return carry

    lax.fori_loop(0, chips, relayed, 0)


def on_device(value_next, income_matrix, block_weights, block_offset, block_count, asset_next, flow):
    tiles = lax.axis_size("skill")
    chips = tiles // 2
    rows, assets, skills = value_next.shape
    tile = skills // tiles
    shocks = income_matrix.shape[0]
    levels, blocks = block_weights.shape[1:3]
    mix = jnp.kron(jnp.eye(rows // shocks, dtype=jnp.float32), income_matrix)
    turned = jnp.transpose(value_next, (1, 0, 2))
    smem = pl.BlockSpec(memory_space=pltpu.SMEM)
    vmem = pl.BlockSpec(memory_space=pltpu.VMEM)
    dma = pltpu.SemaphoreType.DMA
    back = pl.pallas_call(
        functools.partial(fused_kernel, tiles),
        out_shape=jax.ShapeDtypeStruct((tiles, assets, rows, tile), jnp.bfloat16),
        in_specs=[smem, smem, vmem, vmem, vmem, vmem, vmem],
        out_specs=pl.BlockSpec(memory_space=pl.ANY),
        scratch_shapes=[
            pltpu.VMEM((chips, 2, assets, rows, tile), jnp.bfloat16),
            pltpu.VMEM((chips, blocks + 1, assets, rows, tile), jnp.bfloat16),
            pltpu.VMEM((2, tile // STEP, levels * STEP, blocks * tile), jnp.bfloat16),
            pltpu.VMEM((chips, 2, assets, rows, tile), jnp.bfloat16),
            pltpu.VMEM((assets, levels, rows), jnp.float32),
            pltpu.VMEM((assets, levels, rows), jnp.int32),
            pltpu.VMEM((2, levels * STEP, assets * rows), jnp.float32),
            pltpu.VMEM((assets, tile, rows), jnp.float32),
            dma((chips,)),
            dma((chips,)),
            dma((chips,)),
            dma((chips,)),
            dma((chips,)),
            dma((chips,)),
            dma((chips,)),
            dma((chips,)),
            dma((2,)),
            dma,
        ],
        compiler_params=pltpu.CompilerParams(
            collective_id=0, has_side_effects=True, vmem_limit_bytes=48 * 1024 * 1024
        ),
    )(block_offset[0], block_count, mix, turned, block_weights[0], flow, asset_next)
    return jnp.transpose(back, (2, 1, 0, 3)).reshape(rows, assets, skills)


def solution(mesh):
    placed = (
        P("skill", "grp", None),
        P("grp", None),
        P("skill", None, None, None, None),
        P("skill", None, None),
        P("skill", None),
        P(),
        P("grp", None, None),
    )

    def body(value_next, income_matrix, *rest):
        whole = value_next.shape[0] % income_matrix.shape[0] == 0 and mesh.shape["skill"] >= 8
        return (on_device if whole else on_device_split)(value_next, income_matrix, *rest)

    return jax.shard_map(
        body, mesh=mesh, in_specs=placed, out_specs=P("skill", "grp", None), check_vma=False
    )
```
